128 devices in a mesh: growth: 4 (over z), lat: 32 (over x, y, core).
Axes of the slice: x: 4, y: 4, z: 4, core: 2. Of those that a mesh axis runs over, the one named last changes fastest.
Arguments:
- source: float32 [32, 1024, 1024], P('growth', 'lat'), may hold values from -4 to 4
- spacing: float32 [32], P('growth'), may hold values from 0.5 to 2
Outputs:
- potential: float32 [32, 1024, 1024], P('growth', 'lat')
The draws below stay inside these ranges and needn't reach their ends.
All inputs are finite; a program needn't handle non-finite values.
Results may differ from the reference program's by a relative error of at most 0.0003.
Values sent between devices are 32-bit elements; how exact they have to be, the bound alone decides.
No kernel may reach another device: no remote copies, remote signals or barrier semaphores. Data moves between devices by JAX's collectives and lax.ppermute only.
A program may use at most 128 MiB of HBM per device.

```python
import math
import jax
import jax.numpy as jnp
from jax import lax

NX = 1024
NY = 1024
NZ = 32


def draw_source(key, part):
    rough_part = jax.random.truncated_normal(key, -4.0, 4.0, (NZ, NX, NY), jnp.float32)
    return rough_part


def shard_levels(stream_key, dims, pieces, low, largest):
    def one(position, shards_of):
        draws = jax.random.uniform(jax.random.fold_in(jax.random.fold_in(stream_key, 6), position), (shards_of,), jnp.float32, low / len(pieces), largest / len(pieces))
        return jnp.repeat(jnp.exp(draws), dims[position] // shards_of).reshape((-1,) + (1,) * (len(dims) - position - 1))

    loudness = one(*pieces[0])
    for cut in pieces[1:]:
        loudness = loudness * one(*cut)
    return loudness


def setup_inputs(seed: int = 0) -> dict:
    splits = jax.random.split(jax.random.key(seed), 3)
    return {
        "source": draw_source(jax.random.fold_in(splits[2], 71), 0),
        "spacing": jnp.clip(jnp.exp(math.log(2.0) - 1.3862944 * jax.random.uniform(splits[1], (NZ,), jnp.float32) ** shard_levels(splits[1], (NZ,), ((0, 4),), -0.2, 0.2)), 0.5, 2.0),
    }


full_precision = lax.Precision.HIGHEST

def cosine_table(points):
    indices = jnp.arange(points, dtype=jnp.int32)
    phase = (2 * indices[None, :] + 1) * indices[:, None] % (4 * points)
    angle = phase.astype(jnp.float32) * (math.pi / (2.0 * points))
    scale = jnp.where(indices == 0, math.sqrt(1.0 / points), math.sqrt(2.0 / points)).astype(jnp.float32)
    return scale[:, None] * jnp.cos(angle)

def mode_eigenvalue(mode_ids, points):
    sine_half = jnp.sin(mode_ids.astype(jnp.float32) * (math.pi / (2.0 * points)))
    return 4.0 * sine_half * sine_half

def reference(source, spacing):
    table_x = cosine_table(NX)
    table_y = cosine_table(NY)

    def transform_plane(plane):
        inner_part = jnp.dot(table_x, plane, precision=full_precision, preferred_element_type=jnp.float32)
        return jnp.dot(inner_part, table_y.T, precision=full_precision, preferred_element_type=jnp.float32)
    spectral = lax.map(transform_plane, source)
    eigenvalue = mode_eigenvalue(jnp.arange(NX, dtype=jnp.int32), NX)[:, None] + mode_eigenvalue(jnp.arange(NY, dtype=jnp.int32), NY)[None, :]
    padded = jnp.concatenate([jnp.zeros((1,), jnp.float32), spacing, jnp.zeros((1,), jnp.float32)])
    conduct = 2.0 / (padded[:-1] + padded[1:])
    lower_face = conduct[:-1]
    upper_face = conduct[1:]

    def sweep(carried, row_data):
        factor, partial_value = carried
        face_below, face_above, height, spectral_row = row_data
        pivot = face_below + face_above + height * eigenvalue - face_below * factor
        factor = face_above / pivot
        partial_value = (height * spectral_row + face_below * partial_value) / pivot
        return ((factor, partial_value), (factor, partial_value))
    initial = (jnp.zeros((NX, NY), jnp.float32), jnp.zeros((NX, NY), jnp.float32))
    _, (factors, partials) = lax.scan(sweep, initial, (lower_face, upper_face, spacing, spectral))

    def substitute(above_value, row_data):
        factor, partial_value = row_data
        updated = partial_value + factor * above_value
        return (updated, updated)
    _, modal = lax.scan(substitute, jnp.zeros((NX, NY), jnp.float32), (factors, partials), reverse=True)

    def inverse_plane(plane):
        inner_part = jnp.dot(table_x.T, plane, precision=full_precision, preferred_element_type=jnp.float32)
        return jnp.dot(inner_part, table_y, precision=full_precision, preferred_element_type=jnp.float32)
    return lax.map(inverse_plane, modal)
```

```python
import math

import jax
import jax.numpy as jnp
import numpy as np
from jax import lax
from jax.experimental import pallas as pl
from jax.experimental.pallas import tpu as pltpu
from jax.sharding import PartitionSpec as P

ALL = ("growth", "lat")
LANES = 128
SUB = 8


def table_factors(points):
    k = np.arange(points, dtype=np.int64)[:, None]
    j = np.arange(LANES, dtype=np.int64)[None, :]
    angle = ((2 * j + 1) * k % (4 * points)).astype(np.float64) * (math.pi / (2.0 * points))
    scale = np.where(k == 0, math.sqrt(1.0 / points), math.sqrt(2.0 / points))
    tiles = points // LANES
    period = 2 * tiles
    kk = np.arange(period, dtype=np.int64)[:, None]
    t = np.arange(tiles, dtype=np.int64)[None, :]
    turn = (t * kk % period).astype(np.float64) * (math.pi / tiles)
    wide_cos = np.repeat(np.cos(turn), LANES, axis=1)
    wide_sin = np.repeat(np.sin(turn), LANES, axis=1)
    return [
        a.astype(np.float32)
        for a in (scale * np.cos(angle), scale * np.sin(angle), wide_cos, wide_sin)
    ]


def eigenvalues(points):
    sine = np.sin(np.arange(points, dtype=np.float64) * (math.pi / (2.0 * points)))
    return (4.0 * sine * sine).astype(np.float32)


def split(value):
    high = value.astype(jnp.bfloat16)
    low = (value - high.astype(jnp.float32)).astype(jnp.bfloat16)
    return high, low


def product(left, right, dims):
    def one(a, b):
        return lax.dot_general(a, b, (dims, ((), ())), preferred_element_type=jnp.float32)

    return one(left[0], right[0]) + (one(left[0], right[1]) + one(left[1], right[0]))


def forward_y(source, base_cos, base_sin, wide_cos, wide_sin, out, high, low, rows, sem):
    fetch = pltpu.make_async_copy(source, rows, sem)
    fetch.start()
    points = high.shape[0]
    tiles = points // LANES
    period = wide_cos.shape[0]
    wc = wide_cos[...]
    ws = wide_sin[...]

    @pl.loop(0, points // period)
    def _(i):
        at = pl.ds(pl.multiple_of(i * period, period), period)
        bc = jnp.concatenate([base_cos[at, :]] * tiles, axis=1)
        bs = jnp.concatenate([base_sin[at, :]] * tiles, axis=1)
        h, l = split(bc * wc - bs * ws)
        high[at, :] = h
        low[at, :] = l

    fetch.wait()
    data = split(rows[...])
    step = 256
    for i in range(points // step):
        at = pl.ds(i * step, step)
        out[at, :] = product((high[at, :], low[at, :]), data, ((1,), (1,)))


def swap_groups(v, group):
    low_half = group < 2
    even = group % 2 == 0
    t0 = jnp.where(low_half, v[0], pltpu.roll(v[2], 64, 1))
    t2 = jnp.where(low_half, pltpu.roll(v[0], 64, 1), v[2])
    t1 = jnp.where(low_half, v[1], pltpu.roll(v[3], 64, 1))
    t3 = jnp.where(low_half, pltpu.roll(v[1], 64, 1), v[3])
    w0 = jnp.where(even, t0, pltpu.roll(t1, 32, 1))
    w1 = jnp.where(even, pltpu.roll(t0, 96, 1), t1)
    w2 = jnp.where(even, t2, pltpu.roll(t3, 32, 1))
    w3 = jnp.where(even, pltpu.roll(t2, 96, 1), t3)
    return w0, w1, w2, w3


def middle(
    moved, high, low, own, next1, next2, next3, eig_x, eig_y, out, rows, heights, inverse
):
    slab = own.shape[0]
    slabs = 4
    depth = slab * slabs
    lat = moved.shape[0] // slabs
    width = rows.shape[1]
    grow = lax.axis_index("growth")
    rank = grow * lat + lax.axis_index("lat")
    for k, ref in enumerate((own, next1, next2, next3)):
        at = pl.ds(pl.multiple_of(lax.rem(grow + k, slabs) * slab, slab), slab)
        heights[at, :] = ref[...]
    lane = lax.broadcasted_iota(jnp.int32, (SUB, LANES), 1)
    group = lane // 32

    ey = jnp.sum(jnp.where(lane == rank, eig_y[...], 0.0), axis=1, keepdims=True)
    eigen = jnp.broadcast_to(ey, (SUB, width)) + jnp.broadcast_to(eig_x[...], (SUB, width))

    def wide(row):
        return jnp.concatenate([jnp.broadcast_to(row, (SUB, LANES))] * (width // LANES), axis=1)

    h = [heights[z : z + 1, :] for z in range(depth)]
    zero = jnp.zeros_like(h[0])
    padded = [zero] + h + [zero]
    conduct = [2.0 / (padded[i] + padded[i + 1]) for i in range(depth + 1)]
    inv = None
    for z in range(depth):
        pivot = wide(conduct[z] + conduct[z + 1]) + wide(h[z]) * eigen
        if z:
            pivot = pivot - wide(conduct[z] * conduct[z]) * inv
        inv = 1.0 / pivot
        inverse[pl.ds(z * SUB, SUB), :] = inv

    for g in range(slabs):
        for half in range(2):
            for j in range(lat // 4):
                v = [
                    moved[g * lat + 4 * j + i, :, pl.ds(half * LANES, LANES)] for i in range(4)
                ]
                for q, w in enumerate(swap_groups(v, group)):
                    z = g * slab + half * 4 + q
                    rows[pl.ds(z * SUB, SUB), pl.ds(j * LANES, LANES)] = w

    table = (high[...], low[...])
    rows[...] = product(split(rows[...]), table, ((1,), (1,)))

    partial = None
    for z in range(depth):
        at = pl.ds(z * SUB, SUB)
        value = wide(h[z]) * rows[at, :]
        if z:
            value = value + wide(conduct[z]) * partial
        partial = value * inverse[at, :]
        rows[at, :] = partial
    solved = partial
    for z in reversed(range(depth - 1)):
        at = pl.ds(z * SUB, SUB)
        solved = rows[at, :] + wide(conduct[z + 1]) * inverse[at, :] * solved
        rows[at, :] = solved

    rows[...] = product(split(rows[...]), table, ((1,), (0,)))

    for g in range(slabs):
        for half in range(2):
            for j in range(lat // 4):
                w = [
                    rows[
                        pl.ds((g * slab + half * 4 + q) * SUB, SUB), pl.ds(j * LANES, LANES)
                    ]
                    for q in range(4)
                ]
                for i, v in enumerate(swap_groups(w, group)):
                    out[g * lat + 4 * j + i, :, pl.ds(half * LANES, LANES)] = v


def inverse_y(planes, high, low, out, result, sem):
    table = (high[...], low[...])
    flat = planes[...].T
    count = 4
    step = flat.shape[0] // count
    copies = []
    for i in range(count):
        at = pl.ds(i * step, step)
        result[at, :] = product(split(flat[i * step : (i + 1) * step, :]), table, ((1,), (0,)))
        copies.append(pltpu.make_async_copy(result.at[at, :], out.at[at, :], sem.at[i]))
        copies[-1].start()
    for copy in copies:
        copy.wait()


VMEM = pl.BlockSpec(memory_space=pltpu.VMEM)
HBM = pl.BlockSpec(memory_space=pl.ANY)


def shape(*dims, dtype=jnp.float32):
    return jax.ShapeDtypeStruct(dims, dtype)


def solution(mesh):
    slabs = mesh.shape["growth"]
    lat = mesh.shape["lat"]

    def per_device(source, spacing):
        slab, xlocal, width = source.shape
        devices = slabs * lat
        flat = slab * xlocal
        factors = [jnp.asarray(a) for a in table_factors(width)]
        eig = eigenvalues(width)
        eig_x = jnp.asarray(eig[None, :])
        eig_y = jnp.asarray(eig.reshape(devices, SUB).T)
        own = jnp.broadcast_to(spacing[:, None], (slab, LANES))
        others = [
            lax.ppermute(own, "growth", [((j + k) % slabs, j) for j in range(slabs)])
            for k in range(1, slabs)
        ]
        planes, high, low = pl.pallas_call(
            forward_y,
            out_shape=(
                shape(width, flat),
                shape(width, width, dtype=jnp.bfloat16),
                shape(width, width, dtype=jnp.bfloat16),
            ),
            in_specs=[HBM] + [VMEM] * 4,
            out_specs=(VMEM,) * 3,
            scratch_shapes=[pltpu.VMEM((flat, width), jnp.float32), pltpu.SemaphoreType.DMA],
            compiler_params=pltpu.CompilerParams(vmem_limit_bytes=24 << 20),
            name="forward_y",
        )(source.reshape(flat, width), *factors)
        moved = lax.all_to_all(
            planes.reshape(devices, SUB, flat), ALL, 0, 0, tiled=True
        )
        spatial = pl.pallas_call(
            middle,
            out_shape=shape(devices, SUB, flat),
            in_specs=[VMEM] * 9,
            out_specs=VMEM,
            scratch_shapes=[
                pltpu.VMEM((slab * slabs * SUB, width), jnp.float32),
                pltpu.VMEM((slab * slabs, LANES), jnp.float32),
                pltpu.VMEM((slab * slabs * SUB, width), jnp.float32),
            ],
            compiler_params=pltpu.CompilerParams(vmem_limit_bytes=32 << 20),
            name="middle",
        )(moved, high, low, own, *others, eig_x, eig_y)
        returned = lax.all_to_all(spatial, ALL, 0, 0, tiled=True)
        result = pl.pallas_call(
            inverse_y,
            out_shape=shape(flat, width),
            in_specs=[VMEM] * 3,
            out_specs=HBM,
            scratch_shapes=[
                pltpu.VMEM((flat, width), jnp.float32),
                pltpu.SemaphoreType.DMA((4,)),
            ],
            compiler_params=pltpu.CompilerParams(vmem_limit_bytes=24 << 20),
            name="inverse_y",
        )(returned.reshape(width, flat), high, low)
        return result.reshape(slab, xlocal, width)

    return jax.shard_map(
        per_device,
        mesh=mesh,
        in_specs=(P("growth", "lat", None), P("growth")),
        out_specs=P("growth", "lat", None),
        check_vma=False,
    )
```

```python
import math

import jax
import jax.numpy as jnp
import numpy as np
from jax import lax
from jax.experimental import pallas as pl
from jax.experimental.pallas import tpu as pltpu
from jax.sharding import PartitionSpec as P

ALL = ("growth", "lat")
LANES = 128
SUB = 8
GROUP = 32
NT = ((1,), (1,))
NN = ((1,), (0,))


def mode_order(points):
    return np.concatenate([np.arange(0, points, 2), np.arange(1, points, 2)])


def half_table(points):
    k = mode_order(points)[:, None].astype(np.int64)
    j = np.arange(points // 2, dtype=np.int64)[None, :]
    angle = ((2 * j + 1) * k % (4 * points)).astype(np.float64) * (math.pi / (2.0 * points))
    scale = np.where(k == 0, math.sqrt(1.0 / points), math.sqrt(2.0 / points))
    table = (scale * np.cos(angle)).astype(np.float32)
    high = table.astype(jnp.bfloat16)
    low = (table - high.astype(np.float32)).astype(jnp.bfloat16)
    return np.concatenate([high, low], axis=0)


def eigenvalues(points):
    sine = np.sin(mode_order(points).astype(np.float64) * (math.pi / (2.0 * points)))
    return (4.0 * sine * sine).astype(np.float32)


def split(value):
    high = value.astype(jnp.bfloat16)
    low = (value - high.astype(jnp.float32)).astype(jnp.bfloat16)
    return high, low


def product(left, right, dims):
    def one(a, b):
        return lax.dot_general(a, b, (dims, ((), ())), preferred_element_type=jnp.float32)

    return one(left[0], right[0]) + (one(left[0], right[1]) + one(left[1], right[0]))


def parity(table, which):
    n = table.shape[0] // 4
    return (
        table[which * n : (which + 1) * n, :],
        table[(2 + which) * n : (3 + which) * n, :],
    )


def reverse_lanes(value, span):
    lane = lax.broadcasted_iota(jnp.int32, value.shape, 1)
    source = lane // span * span + (span - 1) - lane % span
    return jnp.take_along_axis(value, source, axis=1)


def forward_y(source, table_hbm, out_hbm, rows, table, out, sem, table_sem, out_sem):
    points = rows.shape[1]
    half = points // 2
    tiles = half // LANES
    fetch = pltpu.make_async_copy(source, rows, sem)
    fetch.start()
    tables = []
    for which in range(2):
        for part in range(2):
            at = pl.ds((2 * part + which) * half, half)
            tables.append(
                pltpu.make_async_copy(
                    table_hbm.at[at, :], table.at[at, :], table_sem.at[2 * which + part]
                )
            )
            tables[-1].start()
    fetch.wait()
    first = [rows[:, pl.ds(j * LANES, LANES)] for j in range(tiles)]
    second = [
        reverse_lanes(rows[:, pl.ds((2 * tiles - 1 - j) * LANES, LANES)], LANES)
        for j in range(tiles)
    ]
    folded = (
        split(jnp.concatenate([a + b for a, b in zip(first, second)], axis=1)),
        split(jnp.concatenate([a - b for a, b in zip(first, second)], axis=1)),
    )
    copies = []
    for which in range(2):
        tables[2 * which].wait()
        tables[2 * which + 1].wait()
        at = pl.ds(which * half, half)
        out[at, :] = product(parity(table, which), folded[which], NT)
        copies.append(
            pltpu.make_async_copy(out.at[at, :], out_hbm.at[at, :], out_sem.at[which])
        )
        copies[-1].start()
    for copy in copies:
        copy.wait()


def swap_groups(v, group):
    low_half = group < 2
    even = group % 2 == 0
    t0 = jnp.where(low_half, v[0], pltpu.roll(v[2], 64, 1))
    t2 = jnp.where(low_half, pltpu.roll(v[0], 64, 1), v[2])
    t1 = jnp.where(low_half, v[1], pltpu.roll(v[3], 64, 1))
    t3 = jnp.where(low_half, pltpu.roll(v[1], 64, 1), v[3])
    w0 = jnp.where(even, t0, pltpu.roll(t1, 32, 1))
    w1 = jnp.where(even, pltpu.roll(t0, 96, 1), t1)
    w2 = jnp.where(even, t2, pltpu.roll(t3, 32, 1))
    w3 = jnp.where(even, pltpu.roll(t2, 96, 1), t3)
    return w0, w1, w2, w3


def wide(row, width):
    return jnp.concatenate([jnp.broadcast_to(row, (SUB, LANES))] * (width // LANES), axis=1)


def conductances(h):
    zero = jnp.zeros_like(h[0])
    padded = [zero] + h + [zero]
    return [2.0 / (padded[i] + padded[i + 1]) for i in range(len(h) + 1)]


def fill_pivots(own, next1, next2, next3, eig_x, eig_y, heights, inverse):
    slab = own.shape[0]
    slabs = 4
    depth = slab * slabs
    width = inverse.shape[1]
    grow = lax.axis_index("growth")
    rank = grow * lax.axis_size("lat") + lax.axis_index("lat")
    for k, ref in enumerate((own, next1, next2, next3)):
        at = pl.ds(pl.multiple_of(lax.rem(grow + k, slabs) * slab, slab), slab)
        heights[at, :] = ref[...]
    lane = lax.broadcasted_iota(jnp.int32, (SUB, LANES), 1)
    ey = jnp.sum(jnp.where(lane == rank, eig_y[...], 0.0), axis=1, keepdims=True)
    eigen = jnp.broadcast_to(ey, (SUB, width)) + jnp.broadcast_to(eig_x[...], (SUB, width))
    h = [heights[z : z + 1, :] for z in range(depth)]
    conduct = conductances(h)
    inv = None
    for z in range(depth):
        pivot = wide(conduct[z] + conduct[z + 1], width) + wide(h[z], width) * eigen
        if z:
            pivot = pivot - wide(conduct[z] * conduct[z], width) * inv
        inv = 1.0 / pivot
        inverse[pl.ds(z * SUB, SUB), :] = inv


def middle(
    moved, table, own, next1, next2, next3, eig_x, eig_y, out, rows, heights, inverse
):
    slabs = 4
    fill_pivots(own, next1, next2, next3, eig_x, eig_y, heights, inverse)
    depth = heights.shape[0]
    slab = depth // slabs
    lat = moved.shape[0] // slabs
    width = rows.shape[1]
    half = width // 2
    tiles = half // LANES
    group = lax.broadcasted_iota(jnp.int32, (SUB, LANES), 1) // GROUP
    for g in range(slabs):
        for s in range(2):
            lanes = pl.ds(s * LANES, LANES)
            for j in range(tiles):
                first = swap_groups(
                    [moved[g * lat + 4 * j + i, :, lanes] for i in range(4)], group
                )
                second = swap_groups(
                    [moved[g * lat + lat - 1 - 4 * j - i, :, lanes] for i in range(4)], group
                )
                for q in range(4):
                    z = g * slab + s * 4 + q
                    a = first[q]
                    b = reverse_lanes(second[q], GROUP)
                    at = pl.ds(z * SUB, SUB)
                    rows[at, pl.ds(j * LANES, LANES)] = a + b
                    rows[at, pl.ds(half + j * LANES, LANES)] = a - b
    for which in range(2):
        at = pl.ds(which * half, half)
        rows[:, at] = product(split(rows[:, at]), parity(table, which), NT)

    h = [heights[z : z + 1, :] for z in range(depth)]
    conduct = conductances(h)
    partial = None
    for z in range(depth):
        at = pl.ds(z * SUB, SUB)
        value = wide(h[z], width) * rows[at, :]
        if z:
            value = value + wide(conduct[z], width) * partial
        partial = value * inverse[at, :]
        rows[at, :] = partial
    solved = partial
    for z in reversed(range(depth - 1)):
        at = pl.ds(z * SUB, SUB)
        solved = rows[at, :] + wide(conduct[z + 1], width) * inverse[at, :] * solved
        rows[at, :] = solved

    for which in range(2):
        at = pl.ds(which * half, half)
        rows[:, at] = product(split(rows[:, at]), parity(table, which), NN)
    for g in range(slabs):
        for s in range(2):
            lanes = pl.ds(s * LANES, LANES)
            for j in range(tiles):
                first = []
                second = []
                for q in range(4):
                    at = pl.ds((g * slab + s * 4 + q) * SUB, SUB)
                    a = rows[at, pl.ds(j * LANES, LANES)]
                    b = rows[at, pl.ds(half + j * LANES, LANES)]
                    first.append(a + b)
                    second.append(reverse_lanes(a - b, GROUP))
                for i, v in enumerate(swap_groups(first, group)):
                    out[g * lat + 4 * j + i, :, lanes] = v
                for i, v in enumerate(swap_groups(second, group)):
                    out[g * lat + lat - 1 - 4 * j - i, :, lanes] = v


def inverse_y(planes, table, out, result, sem):
    half = table.shape[1]
    tiles = half // LANES
    flat = planes.shape[1]
    count = flat // LANES
    copies = []
    for i in range(count):
        at = pl.ds(i * LANES, LANES)
        even, odd = (
            product(
                split(planes[pl.ds(which * half, half), at].T), parity(table, which), NN
            )
            for which in range(2)
        )
        result[at, pl.ds(0, half)] = even + odd
        for j in range(tiles):
            lanes = slice(j * LANES, (j + 1) * LANES)
            result[at, pl.ds((2 * tiles - 1 - j) * LANES, LANES)] = reverse_lanes(
                even[:, lanes] - odd[:, lanes], LANES
            )
        copies.append(pltpu.make_async_copy(result.at[at, :], out.at[at, :], sem.at[i]))
        copies[-1].start()
    for copy in copies:
        copy.wait()


VMEM = pl.BlockSpec(memory_space=pltpu.VMEM)
HBM = pl.BlockSpec(memory_space=pltpu.HBM)


def shape(*dims, dtype=jnp.float32):
    return jax.ShapeDtypeStruct(dims, dtype)


def limit(mebibytes):
    return pltpu.CompilerParams(vmem_limit_bytes=mebibytes << 20)


def solution(mesh):
    slabs = mesh.shape["growth"]
    lat = mesh.shape["lat"]

    def per_device(source, spacing):
        slab, xlocal, width = source.shape
        devices = slabs * lat
        flat = slab * xlocal
        half = width // 2
        depth = slab * slabs
        table = jnp.asarray(half_table(width))
        eig = eigenvalues(width)
        eig_x = jnp.asarray(eig[None, :])
        eig_y = jnp.asarray(eig.reshape(devices, SUB).T)
        own = jnp.broadcast_to(spacing[:, None], (slab, LANES))
        others = [
            lax.ppermute(own, "growth", [((j + k) % slabs, j) for j in range(slabs)])
            for k in range(1, slabs)
        ]
        planes = pl.pallas_call(
            forward_y,
            out_shape=shape(width, flat),
            in_specs=[HBM, HBM],
            out_specs=HBM,
            scratch_shapes=[
                pltpu.VMEM((flat, width), jnp.float32),
                pltpu.VMEM((2 * width, half), jnp.bfloat16),
                pltpu.VMEM((width, flat), jnp.float32),
                pltpu.SemaphoreType.DMA,
                pltpu.SemaphoreType.DMA((4,)),
                pltpu.SemaphoreType.DMA((2,)),
            ],
            compiler_params=pltpu.CompilerParams(vmem_limit_bytes=67043328),
            name="forward_y",
        )(source.reshape(flat, width), table)
        moved = lax.all_to_all(planes.reshape(devices, SUB, flat), ALL, 0, 0, tiled=True)
        spatial = pl.pallas_call(
            middle,
            out_shape=shape(devices, SUB, flat),
            in_specs=[VMEM] * 8,
            out_specs=VMEM,
            scratch_shapes=[
                pltpu.VMEM((depth * SUB, width), jnp.float32),
                pltpu.VMEM((depth, LANES), jnp.float32),
                pltpu.VMEM((depth * SUB, width), jnp.float32),
            ],
            compiler_params=limit(24),
            name="middle",
        )(moved, table, own, *others, eig_x, eig_y)
        returned = lax.all_to_all(spatial, ALL, 0, 0, tiled=True)
        result = pl.pallas_call(
            inverse_y,
            out_shape=shape(flat, width),
            in_specs=[VMEM] * 2,
            out_specs=HBM,
            scratch_shapes=[
                pltpu.VMEM((flat, width), jnp.float32),
                pltpu.SemaphoreType.DMA((flat // LANES,)),
            ],
            compiler_params=limit(24),
            name="inverse_y",
        )(returned.reshape(width, flat), table)
        return result.reshape(slab, xlocal, width)

    return jax.shard_map(
        per_device,
        mesh=mesh,
        in_specs=(P("growth", "lat", None), P("growth")),
        out_specs=P("growth", "lat", None),
        check_vma=False,
    )
```

```python
import math

import jax
import jax.numpy as jnp
import numpy as np
from jax import lax
from jax.experimental import pallas as pl
from jax.experimental.pallas import tpu as pltpu
from jax.sharding import PartitionSpec as P

ALL = ("growth", "lat")
LANES = 128
SUB = 8
GROUP = 32
NT = ((1,), (1,))
NN = ((1,), (0,))


def mode_order(points):
    return np.concatenate([np.arange(0, points, 2), np.arange(1, points, 2)])


def half_table(points):
    k = mode_order(points)[:, None].astype(np.int64)
    j = np.arange(points // 2, dtype=np.int64)[None, :]
    angle = ((2 * j + 1) * k % (4 * points)).astype(np.float64) * (math.pi / (2.0 * points))
    scale = np.where(k == 0, math.sqrt(1.0 / points), math.sqrt(2.0 / points))
    table = (scale * np.cos(angle)).astype(np.float32)
    high = table.astype(jnp.bfloat16)
    low = (table - high.astype(np.float32)).astype(jnp.bfloat16)
    return np.concatenate([high, low], axis=0)


def quarter_sine(angle):
    square = angle * angle
    value = 1.0 - square * (1.0 / 156.0)
    for divisor in (110.0, 72.0, 42.0, 20.0, 6.0):
        value = 1.0 - square * value * (1.0 / divisor)
    return angle * value


def eigenvalue(slot, points):
    half = points // 2
    mode = jnp.where(slot < half, 2 * slot, 2 * (slot - half) + 1)
    sine = quarter_sine(mode.astype(jnp.float32) * (math.pi / (2.0 * points)))
    return 4.0 * sine * sine


def split(value):
    high = value.astype(jnp.bfloat16)
    low = (value - high.astype(jnp.float32)).astype(jnp.bfloat16)
    return high, low


def product(left, right, dims):
    def one(a, b):
        return lax.dot_general(a, b, (dims, ((), ())), preferred_element_type=jnp.float32)

    return one(left[0], right[0]) + (one(left[0], right[1]) + one(left[1], right[0]))


def shared(left, right, dims):
    def one(a, b):
        return lax.dot_general(a, b, (dims, ((), ())), preferred_element_type=jnp.float32)

    count = left[0].shape[0]
    both = one(jnp.concatenate(left, axis=0), right[0])
    return both[:count] + (one(left[0], right[1]) + both[count:])


def parity(table, which):
    n = table.shape[0] // 4
    return (
        table[which * n : (which + 1) * n, :],
        table[(2 + which) * n : (3 + which) * n, :],
    )


def reverse_lanes(value, span):
    lane = lax.broadcasted_iota(jnp.int32, value.shape, 1)
    source = lane // span * span + (span - 1) - lane % span
    return jnp.take_along_axis(value, source, axis=1)


def forward_y(source, table_hbm, out_hbm, rows, table, out, sem, table_sem, out_sem):
    flat, points = rows.shape
    half = points // 2
    tiles = half // LANES
    pieces = 4
    step = points // pieces
    fetch = pltpu.make_async_copy(source, rows, sem)
    fetch.start()

    def table_copy(i):
        at = pl.ds(pl.multiple_of((i % 2) * points + (i // 2) * half, half), half)
        return pltpu.make_async_copy(table_hbm.at[at, :], table.at[at, :], table_sem.at[i])

    @pl.loop(0, 4)
    def _(i):
        table_copy(i).start()

    fetch.wait()
    first = [rows[:, pl.ds(j * LANES, LANES)] for j in range(tiles)]
    second = [
        reverse_lanes(rows[:, pl.ds((2 * tiles - 1 - j) * LANES, LANES)], LANES)
        for j in range(tiles)
    ]
    folded = (
        split(jnp.concatenate([a + b for a, b in zip(first, second)], axis=1)),
        split(jnp.concatenate([a - b for a, b in zip(first, second)], axis=1)),
    )
    copies = []
    for i in range(pieces):
        which = i * 2 // pieces
        if i % (pieces // 2) == 0:
            table_copy(2 * which).wait()
            table_copy(2 * which + 1).wait()
        at = pl.ds(i * step, step)
        low = pl.ds(points + i * step, step)
        out[at, :] = product((table[at, :], table[low, :]), folded[which], NT)
        copies.append(pltpu.make_async_copy(out.at[at, :], out_hbm.at[at, :], out_sem.at[i]))
        copies[-1].start()
    for copy in copies:
        copy.wait()


def permute(value, source):
    return jnp.take_along_axis(value, source, axis=1)


def exchange(a, b, keep, source, turn=None):
    moved = permute(jnp.where(keep, b, a), source)
    if turn is None:
        return jnp.where(keep, a, moved), jnp.where(keep, moved, b)
    kept = permute(jnp.where(keep, a, b), turn)
    return jnp.where(keep, kept, moved), jnp.where(keep, moved, kept)


def swap_groups(v, lane, reverse):
    keep = lane < 2 * GROUP
    t0, t2 = exchange(v[0], v[2], keep, lane ^ (2 * GROUP))
    t1, t3 = exchange(v[1], v[3], keep, lane ^ (2 * GROUP))
    keep = lane // GROUP % 2 == 0
    source, turn = lane ^ GROUP, None
    if reverse:
        source, turn = lane ^ (2 * GROUP - 1), lane ^ (GROUP - 1)
    w0, w1 = exchange(t0, t1, keep, source, turn)
    w2, w3 = exchange(t2, t3, keep, source, turn)
    return w0, w1, w2, w3


def wide(row, width):
    return jnp.concatenate([jnp.broadcast_to(row, (SUB, LANES))] * (width // LANES), axis=1)


def conductances(h):
    zero = jnp.zeros_like(h[0])
    padded = [zero] + h + [zero]
    return [2.0 / (padded[i] + padded[i + 1]) for i in range(len(h) + 1)]


def pivots(own, next1, next2, next3, heights, inverse):
    slab = own.shape[0]
    slabs = 4
    depth = slab * slabs
    width = inverse.shape[1]
    grow = lax.axis_index("growth")
    rank = grow * lax.axis_size("lat") + lax.axis_index("lat")
    for k, ref in enumerate((own, next1, next2, next3)):
        at = pl.ds(pl.multiple_of(lax.rem(grow + k, slabs) * slab, slab), slab)
        heights[at, :] = ref[...]
    row = lax.broadcasted_iota(jnp.int32, (SUB, LANES), 0) + rank * SUB
    column = lax.broadcasted_iota(jnp.int32, (SUB, width), 1)
    ey = jnp.concatenate([eigenvalue(row, width)] * (width // LANES), axis=1)
    total = ey + eigenvalue(column, width)
    h = [heights[z : z + 1, :] for z in range(depth)]
    conduct = conductances(h)
    inv = None
    for z in range(depth):
        pivot = wide(conduct[z] + conduct[z + 1], width) + wide(h[z], width) * total
        if z:
            pivot = pivot - wide(conduct[z] * conduct[z], width) * inv
        inv = 1.0 / pivot
        inverse[pl.ds(z * SUB, SUB), :] = inv


def middle(
    moved, table, own, next1, next2, next3, out, rows, heights, inverse
):
    slabs = 4
    pivots(own, next1, next2, next3, heights, inverse)
    depth = heights.shape[0]
    slab = depth // slabs
    lat = moved.shape[0] // slabs
    width = rows.shape[1]
    half = width // 2
    tiles = half // LANES
    lane = lax.broadcasted_iota(jnp.int32, (SUB, LANES), 1)
    chunks = 2
    span = half // chunks
    blocks = [(g, s) for g in range(slabs) for s in range(2)]

    def part(which, high):
        return pl.ds((0 if high else width) + which * half, half)

    sums = [None, None]
    for c in range(chunks):
        for g, s in blocks:
            lanes = pl.ds(s * LANES, LANES)
            for j in range(c * tiles // chunks, (c + 1) * tiles // chunks):
                first = swap_groups(
                    [moved[g * lat + 4 * j + i, :, lanes] for i in range(4)], lane, False
                )
                second = swap_groups(
                    [moved[g * lat + lat - 1 - 4 * j - i, :, lanes] for i in range(4)],
                    lane,
                    True,
                )
                for q in range(4):
                    at = pl.ds((g * slab + s * 4 + q) * SUB, SUB)
                    rows[at, pl.ds(j * LANES, LANES)] = first[q] + second[q]
                    rows[at, pl.ds(half + j * LANES, LANES)] = first[q] - second[q]
        at = pl.ds(c * span, span)
        for which in range(2):
            data = split(rows[:, pl.ds(which * half + c * span, span)])
            value = shared(data, (table[part(which, 1), at], table[part(which, 0), at]), NT)
            sums[which] = value if c == 0 else sums[which] + value

    h = [heights[z : z + 1, :] for z in range(depth)]
    conduct = conductances(h)

    def solve(which):
        lanes = pl.ds(which * half, half)
        partial = None
        for z in range(depth):
            at = pl.ds(z * SUB, SUB)
            value = wide(h[z], half) * rows[at, lanes]
            if z:
                value = value + wide(conduct[z], half) * partial
            partial = value * inverse[at, lanes]
            rows[at, lanes] = partial
        solved = partial
        for z in reversed(range(depth - 1)):
            at = pl.ds(z * SUB, SUB)
            solved = rows[at, lanes] + wide(conduct[z + 1], half) * inverse[at, lanes] * solved
            rows[at, lanes] = solved

    data = []
    for which in range(2):
        rows[:, pl.ds(which * half, half)] = sums[which]
    for which in range(2):
        solve(which)
        data.append(split(rows[:, pl.ds(which * half, half)]))
    for c in range(chunks):
        at = pl.ds(c * span, span)
        even, odd = (
            shared(data[which], (table[part(which, 1), at], table[part(which, 0), at]), NN)
            for which in range(2)
        )
        total, rest = even + odd, even - odd
        for g, s in blocks:
            lanes = pl.ds(s * LANES, LANES)
            for j in range(tiles // chunks):
                where = [
                    slice((g * slab + s * 4 + q) * SUB, (g * slab + s * 4 + q + 1) * SUB)
                    for q in range(4)
                ]
                cols = slice(j * LANES, (j + 1) * LANES)
                base = 4 * (c * tiles // chunks + j)
                for i, v in enumerate(swap_groups([total[w, cols] for w in where], lane, False)):
                    out[g * lat + base + i, :, lanes] = v
                for i, v in enumerate(swap_groups([rest[w, cols] for w in where], lane, True)):
                    out[g * lat + lat - 1 - base - i, :, lanes] = v


def inverse_y(planes, table, out, result, sem):
    points = planes.shape[0]
    half = points // 2
    chunks = 2
    span = half // chunks
    tiles = span // LANES
    data = [split(planes[pl.ds(which * half, half), :].T) for which in range(2)]
    copies = []

    def send(at):
        copies.append(
            pltpu.make_async_copy(result.at[:, at], out.at[:, at], sem.at[len(copies)])
        )
        copies[-1].start()

    for c in range(chunks):
        at = pl.ds(c * span, span)
        even, odd = (
            shared(
                data[which],
                (
                    table[pl.ds(which * half, half), at],
                    table[pl.ds(points + which * half, half), at],
                ),
                NN,
            )
            for which in range(2)
        )
        result[:, at] = even + odd
        send(at)
        rest = even - odd
        mirror = points - (c + 1) * span
        for j in range(tiles):
            lanes = slice((tiles - 1 - j) * LANES, (tiles - j) * LANES)
            result[:, pl.ds(mirror + j * LANES, LANES)] = reverse_lanes(rest[:, lanes], LANES)
        send(pl.ds(mirror, span))
    for copy in copies:
        copy.wait()


VMEM = pl.BlockSpec(memory_space=pltpu.VMEM)
HBM = pl.BlockSpec(memory_space=pltpu.HBM)


def shape(*dims, dtype=jnp.float32):
    return jax.ShapeDtypeStruct(dims, dtype)


FULL = 67043328


def limit(size):
    return pltpu.CompilerParams(vmem_limit_bytes=size)


def solution(mesh):
    slabs = mesh.shape["growth"]
    lat = mesh.shape["lat"]

    def per_device(source, spacing):
        slab, xlocal, width = source.shape
        devices = slabs * lat
        flat = slab * xlocal
        half = width // 2
        depth = slab * slabs
        table = jnp.asarray(half_table(width))
        own = jnp.broadcast_to(spacing[:, None], (slab, LANES))
        others = [
            lax.ppermute(own, "growth", [((j + k) % slabs, j) for j in range(slabs)])
            for k in range(1, slabs)
        ]
        planes = pl.pallas_call(
            forward_y,
            out_shape=shape(width, flat),
            in_specs=[HBM, HBM],
            out_specs=HBM,
            scratch_shapes=[
                pltpu.VMEM((flat, width), jnp.float32),
                pltpu.VMEM((2 * width, half), jnp.bfloat16),
                pltpu.VMEM((width, flat), jnp.float32),
                pltpu.SemaphoreType.DMA,
                pltpu.SemaphoreType.DMA((4,)),
                pltpu.SemaphoreType.DMA((4,)),
            ],
            compiler_params=limit(FULL),
            name="forward_y",
        )(source.reshape(flat, width), table)
        moved = lax.all_to_all(planes.reshape(devices, SUB, flat), ALL, 0, 0, tiled=True)
        spatial = pl.pallas_call(
            middle,
            out_shape=shape(devices, SUB, flat),
            in_specs=[VMEM] * 6,
            out_specs=VMEM,
            scratch_shapes=[
                pltpu.VMEM((depth * SUB, width), jnp.float32),
                pltpu.VMEM((depth, LANES), jnp.float32),
                pltpu.VMEM((depth * SUB, width), jnp.float32),
            ],
            compiler_params=limit(24 << 20),
            name="middle",
        )(moved, table, own, *others)
        returned = lax.all_to_all(spatial, ALL, 0, 0, tiled=True)
        result = pl.pallas_call(
            inverse_y,
            out_shape=shape(flat, width),
            in_specs=[VMEM] * 2,
            out_specs=HBM,
            scratch_shapes=[
                pltpu.VMEM((flat, width), jnp.float32),
                pltpu.SemaphoreType.DMA((4,)),
            ],
            compiler_params=limit(24 << 20),
            name="inverse_y",
        )(returned.reshape(width, flat), table)
        return result.reshape(slab, xlocal, width)

    return jax.shard_map(
        per_device,
        mesh=mesh,
        in_specs=(P("growth", "lat", None), P("growth")),
        out_specs=P("growth", "lat", None),
        check_vma=False,
    )
```

```python
import math

import jax
import jax.numpy as jnp
import numpy as np
from jax import lax
from jax.experimental import pallas as pl
from jax.experimental.pallas import tpu as pltpu
from jax.sharding import PartitionSpec as P

ALL = ("growth", "lat")
LANES = 128
SUB = 8
GROUP = 32
NT = ((1,), (1,))
NN = ((1,), (0,))


def mode_order(points):
    return np.concatenate([np.arange(0, points, 2), np.arange(1, points, 2)])


def half_table(points):
    k = mode_order(points)[:, None].astype(np.int64)
    j = np.arange(points // 2, dtype=np.int64)[None, :]
    angle = ((2 * j + 1) * k % (4 * points)).astype(np.float64) * (math.pi / (2.0 * points))
    scale = np.where(k == 0, math.sqrt(1.0 / points), math.sqrt(2.0 / points))
    table = (scale * np.cos(angle)).astype(np.float32)
    high = table.astype(jnp.bfloat16)
    low = (table - high.astype(np.float32)).astype(jnp.bfloat16)
    return np.concatenate([high, low], axis=0)


def quarter_sine(angle):
    square = angle * angle
    value = 1.0 - square * (1.0 / 156.0)
    for divisor in (110.0, 72.0, 42.0, 20.0, 6.0):
        value = 1.0 - square * value * (1.0 / divisor)
    return angle * value


def eigenvalue(slot, points):
    half = points // 2
    mode = jnp.where(slot < half, 2 * slot, 2 * (slot - half) + 1)
    sine = quarter_sine(mode.astype(jnp.float32) * (math.pi / (2.0 * points)))
    return 4.0 * sine * sine


def split(value):
    high = value.astype(jnp.bfloat16)
    low = (value - high.astype(jnp.float32)).astype(jnp.bfloat16)
    return high, low


def product(left, right, dims):
    def one(a, b):
        return lax.dot_general(a, b, (dims, ((), ())), preferred_element_type=jnp.float32)

    return one(left[0], right[0]) + (one(left[0], right[1]) + one(left[1], right[0]))


def shared(left, right, dims):
    def one(a, b):
        return lax.dot_general(a, b, (dims, ((), ())), preferred_element_type=jnp.float32)

    count = left[0].shape[0]
    both = one(jnp.concatenate(left, axis=0), right[0])
    return both[:count] + (one(left[0], right[1]) + both[count:])


def parity(table, which):
    n = table.shape[0] // 4
    return (
        table[which * n : (which + 1) * n, :],
        table[(2 + which) * n : (3 + which) * n, :],
    )


def reverse_lanes(value, span):
    lane = lax.broadcasted_iota(jnp.int32, value.shape, 1)
    source = lane // span * span + (span - 1) - lane % span
    return jnp.take_along_axis(value, source, axis=1)


def forward_y(source, table_hbm, out_hbm, rows, table, out, sem, table_sem, out_sem):
    flat, points = rows.shape
    half = points // 2
    tiles = half // LANES
    pieces = 4
    step = points // pieces
    fetch = pltpu.make_async_copy(source, rows, sem)
    fetch.start()

    def table_copy(i):
        at = pl.ds(pl.multiple_of((i % 2) * points + (i // 2) * half, half), half)
        return pltpu.make_async_copy(table_hbm.at[at, :], table.at[at, :], table_sem.at[i])

    @pl.loop(0, 4)
    def _(i):
        table_copy(i).start()

    fetch.wait()
    first = [rows[:, pl.ds(j * LANES, LANES)] for j in range(tiles)]
    second = [
        reverse_lanes(rows[:, pl.ds((2 * tiles - 1 - j) * LANES, LANES)], LANES)
        for j in range(tiles)
    ]
    folded = (
        split(jnp.concatenate([a + b for a, b in zip(first, second)], axis=1)),
        split(jnp.concatenate([a - b for a, b in zip(first, second)], axis=1)),
    )
    copies = []
    for i in range(pieces):
        which = i * 2 // pieces
        if i % (pieces // 2) == 0:
            table_copy(2 * which).wait()
            table_copy(2 * which + 1).wait()
        at = pl.ds(i * step, step)
        low = pl.ds(points + i * step, step)
        out[at, :] = product((table[at, :], table[low, :]), folded[which], NT)
        copies.append(pltpu.make_async_copy(out.at[at, :], out_hbm.at[at, :], out_sem.at[i]))
        copies[-1].start()
    for copy in copies:
        copy.wait()


def permute(value, source):
    return jnp.take_along_axis(value, source, axis=1)


def exchange(a, b, keep, source, turn=None):
    moved = jnp.where(keep, b, a)
    moved = pltpu.roll(moved, LANES // 2, 1) if source is None else permute(moved, source)
    if turn is None:
        return jnp.where(keep, a, moved), jnp.where(keep, moved, b)
    kept = permute(jnp.where(keep, a, b), turn)
    return jnp.where(keep, kept, moved), jnp.where(keep, moved, kept)


def swap_groups(v, lane, reverse):
    keep = lane < 2 * GROUP
    t0, t2 = exchange(v[0], v[2], keep, None)
    t1, t3 = exchange(v[1], v[3], keep, None)
    keep = lane // GROUP % 2 == 0
    w = exchange(t0, t1, keep, lane ^ GROUP) + exchange(t2, t3, keep, lane ^ GROUP)
    if reverse:
        w = tuple(permute(x, lane ^ (GROUP - 1)) for x in w)
    return w


def wide(row, width):
    return jnp.concatenate([jnp.broadcast_to(row, (SUB, LANES))] * (width // LANES), axis=1)


def conductances(h):
    zero = jnp.zeros_like(h[0])
    padded = [zero] + h + [zero]
    return [2.0 / (padded[i] + padded[i + 1]) for i in range(len(h) + 1)]


def pivots(own, next1, next2, next3, heights, inverse):
    slab = own.shape[0]
    slabs = 4
    depth = slab * slabs
    width = inverse.shape[1]
    grow = lax.axis_index("growth")
    rank = grow * lax.axis_size("lat") + lax.axis_index("lat")
    for k, ref in enumerate((own, next1, next2, next3)):
        at = pl.ds(pl.multiple_of(lax.rem(grow + k, slabs) * slab, slab), slab)
        heights[at, :] = ref[...]
    row = lax.broadcasted_iota(jnp.int32, (SUB, LANES), 0) + rank * SUB
    column = lax.broadcasted_iota(jnp.int32, (SUB, width), 1)
    ey = jnp.concatenate([eigenvalue(row, width)] * (width // LANES), axis=1)
    total = ey + eigenvalue(column, width)
    h = [heights[z : z + 1, :] for z in range(depth)]
    conduct = conductances(h)
    inv = None
    for z in range(depth):
        pivot = wide(conduct[z] + conduct[z + 1], width) + wide(h[z], width) * total
        if z:
            pivot = pivot - wide(conduct[z] * conduct[z], width) * inv
        inv = 1.0 / pivot
        inverse[pl.ds(z * SUB, SUB), :] = inv


def middle(
    moved, table, own, next1, next2, next3, out, rows, modal, heights, inverse
):
    slabs = 4
    pivots(own, next1, next2, next3, heights, inverse)
    depth = heights.shape[0]
    slab = depth // slabs
    lat = moved.shape[0] // slabs
    width = rows.shape[1]
    half = width // 2
    tiles = half // LANES
    lane = lax.broadcasted_iota(jnp.int32, (SUB, LANES), 1)
    chunks = 2
    span = half // chunks
    blocks = [(g, s) for g in range(slabs) for s in range(2)]

    def part(which, high):
        return pl.ds((0 if high else width) + which * half, half)

    for c in range(chunks):
        for g, s in blocks:
            lanes = pl.ds(s * LANES, LANES)
            for j in range(c * tiles // chunks, (c + 1) * tiles // chunks):
                first = swap_groups(
                    [moved[g * lat + 4 * j + i, :, lanes] for i in range(4)], lane, False
                )
                second = swap_groups(
                    [moved[g * lat + lat - 1 - 4 * j - i, :, lanes] for i in range(4)],
                    lane,
                    True,
                )
                for q in range(4):
                    at = pl.ds((g * slab + s * 4 + q) * SUB, SUB)
                    rows[at, pl.ds(j * LANES, LANES)] = first[q] + second[q]
                    rows[at, pl.ds(half + j * LANES, LANES)] = first[q] - second[q]
        at = pl.ds(c * span, span)
        for which in range(2):
            data = split(rows[:, pl.ds(which * half + c * span, span)])
            value = shared(data, (table[part(which, 1), at], table[part(which, 0), at]), NT)
            to = pl.ds(which * half, half)
            modal[:, to] = value if c == 0 else modal[:, to] + value

    h = [heights[z : z + 1, :] for z in range(depth)]
    conduct = conductances(h)

    def solve(which):
        lanes = pl.ds(which * half, half)
        partial = None
        for z in range(depth):
            at = pl.ds(z * SUB, SUB)
            value = wide(h[z], half) * modal[at, lanes]
            if z:
                value = value + wide(conduct[z], half) * partial
            partial = value * inverse[at, lanes]
            modal[at, lanes] = partial
        solved = partial
        for z in reversed(range(depth - 1)):
            at = pl.ds(z * SUB, SUB)
            solved = modal[at, lanes] + wide(conduct[z + 1], half) * inverse[at, lanes] * solved
            modal[at, lanes] = solved

    def inverse_x(which, data, c):
        at = pl.ds(c * span, span)
        rows[:, pl.ds(which * half + c * span, span)] = shared(
            data, (table[part(which, 1), at], table[part(which, 0), at]), NN
        )

    solve(0)
    even = split(modal[:, pl.ds(0, half)])
    for c in range(chunks):
        inverse_x(0, even, c)
    solve(1)
    odd = split(modal[:, pl.ds(half, half)])
    for c in range(chunks):
        inverse_x(1, odd, c)
        for g, s in blocks:
            lanes = pl.ds(s * LANES, LANES)
            for j in range(c * tiles // chunks, (c + 1) * tiles // chunks):
                first = []
                second = []
                for q in range(4):
                    where = pl.ds((g * slab + s * 4 + q) * SUB, SUB)
                    a = rows[where, pl.ds(j * LANES, LANES)]
                    b = rows[where, pl.ds(half + j * LANES, LANES)]
                    first.append(a + b)
                    second.append(a - b)
                for i, v in enumerate(swap_groups(first, lane, False)):
                    out[g * lat + 4 * j + i, :, lanes] = v
                for i, v in enumerate(swap_groups(second, lane, True)):
                    out[g * lat + lat - 1 - 4 * j - i, :, lanes] = v


def inverse_y(planes, table, out, result, sem):
    points = planes.shape[0]
    half = points // 2
    chunks = 2
    span = half // chunks
    tiles = span // LANES
    data = [split(planes[pl.ds(which * half, half), :].T) for which in range(2)]
    copies = []

    def send(at):
        copies.append(
            pltpu.make_async_copy(result.at[:, at], out.at[:, at], sem.at[len(copies)])
        )
        copies[-1].start()

    for c in range(chunks):
        at = pl.ds(c * span, span)
        even, odd = (
            shared(
                data[which],
                (
                    table[pl.ds(which * half, half), at],
                    table[pl.ds(points + which * half, half), at],
                ),
                NN,
            )
            for which in range(2)
        )
        result[:, at] = even + odd
        send(at)
        rest = even - odd
        mirror = points - (c + 1) * span
        for j in range(tiles):
            lanes = slice((tiles - 1 - j) * LANES, (tiles - j) * LANES)
            result[:, pl.ds(mirror + j * LANES, LANES)] = reverse_lanes(rest[:, lanes], LANES)
        send(pl.ds(mirror, span))
    for copy in copies:
        copy.wait()


VMEM = pl.BlockSpec(memory_space=pltpu.VMEM)
HBM = pl.BlockSpec(memory_space=pltpu.HBM)


def shape(*dims, dtype=jnp.float32):
    return jax.ShapeDtypeStruct(dims, dtype)


FULL = 67043328


def limit(size):
    return pltpu.CompilerParams(vmem_limit_bytes=size)


def solution(mesh):
    slabs = mesh.shape["growth"]
    lat = mesh.shape["lat"]

    def per_device(source, spacing):
        slab, xlocal, width = source.shape
        devices = slabs * lat
        flat = slab * xlocal
        half = width // 2
        depth = slab * slabs
        table = jnp.asarray(half_table(width))
        own = jnp.broadcast_to(spacing[:, None], (slab, LANES))
        others = [
            lax.ppermute(own, "growth", [((j + k) % slabs, j) for j in range(slabs)])
            for k in range(1, slabs)
        ]
        planes = pl.pallas_call(
            forward_y,
            out_shape=shape(width, flat),
            in_specs=[HBM, HBM],
            out_specs=HBM,
            scratch_shapes=[
                pltpu.VMEM((flat, width), jnp.float32),
                pltpu.VMEM((2 * width, half), jnp.bfloat16),
                pltpu.VMEM((width, flat), jnp.float32),
                pltpu.SemaphoreType.DMA,
                pltpu.SemaphoreType.DMA((4,)),
                pltpu.SemaphoreType.DMA((4,)),
            ],
            compiler_params=limit(FULL),
            name="forward_y",
        )(source.reshape(flat, width), table)
        moved = lax.all_to_all(planes.reshape(devices, SUB, flat), ALL, 0, 0, tiled=True)
        spatial = pl.pallas_call(
            middle,
            out_shape=shape(devices, SUB, flat),
            in_specs=[VMEM] * 6,
            out_specs=VMEM,
            scratch_shapes=[
                pltpu.VMEM((depth * SUB, width), jnp.float32),
                pltpu.VMEM((depth * SUB, width), jnp.float32),
                pltpu.VMEM((depth, LANES), jnp.float32),
                pltpu.VMEM((depth * SUB, width), jnp.float32),
            ],
            compiler_params=limit(24 << 20),
            name="middle",
        )(moved, table, own, *others)
        returned = lax.all_to_all(spatial, ALL, 0, 0, tiled=True)
        result = pl.pallas_call(
            inverse_y,
            out_shape=shape(flat, width),
            in_specs=[VMEM] * 2,
            out_specs=HBM,
            scratch_shapes=[
                pltpu.VMEM((flat, width), jnp.float32),
                pltpu.SemaphoreType.DMA((4,)),
            ],
            compiler_params=limit(24 << 20),
            name="inverse_y",
        )(returned.reshape(width, flat), table)
        return result.reshape(slab, xlocal, width)

    return jax.shard_map(
        per_device,
        mesh=mesh,
        in_specs=(P("growth", "lat", None), P("growth")),
        out_specs=P("growth", "lat", None),
        check_vma=False,
    )
```

```python
import math

import jax
import jax.numpy as jnp
import numpy as np
from jax import lax
from jax.experimental import pallas as pl
from jax.experimental.pallas import tpu as pltpu
from jax.sharding import PartitionSpec as P

ALL = ("growth", "lat")
LANES = 128
SUB = 8
GROUP = 32
NT = ((1,), (1,))
NN = ((1,), (0,))


def mode_order(points):
    return np.concatenate(
        [np.arange(0, points, 4), np.arange(2, points, 4), np.arange(1, points, 2)]
    )


def part_table(points, modes, columns):
    k = modes[:, None].astype(np.int64)
    j = np.arange(columns, dtype=np.int64)[None, :]
    angle = ((2 * j + 1) * k % (4 * points)).astype(np.float64) * (math.pi / (2.0 * points))
    scale = np.where(k == 0, math.sqrt(1.0 / points), math.sqrt(2.0 / points))
    table = (scale * np.cos(angle)).astype(np.float32)
    high = table.astype(jnp.bfloat16)
    low = (table - high.astype(np.float32)).astype(jnp.bfloat16)
    return np.concatenate([high, low], axis=0)


def tables(points):
    modes = mode_order(points)
    half = points // 2
    return part_table(points, modes[:half], half // 2), part_table(points, modes[half:], half)


def quarter_sine(angle):
    square = angle * angle
    value = 1.0 - square * (1.0 / 156.0)
    for divisor in (110.0, 72.0, 42.0, 20.0, 6.0):
        value = 1.0 - square * value * (1.0 / divisor)
    return angle * value


def eigenvalue(slot, points):
    half = points // 2
    quarter = points // 4
    even = jnp.where(slot < quarter, 4 * slot, 4 * (slot - quarter) + 2)
    mode = jnp.where(slot < half, even, 2 * (slot - half) + 1)
    sine = quarter_sine(mode.astype(jnp.float32) * (math.pi / (2.0 * points)))
    return 4.0 * sine * sine


def split(value):
    high = value.astype(jnp.bfloat16)
    low = (value - high.astype(jnp.float32)).astype(jnp.bfloat16)
    return high, low


def product(left, right, dims):
    def one(a, b):
        return lax.dot_general(a, b, (dims, ((), ())), preferred_element_type=jnp.float32)

    return one(left[0], right[0]) + (one(left[0], right[1]) + one(left[1], right[0]))


def shared(left, right, dims):
    def one(a, b):
        return lax.dot_general(a, b, (dims, ((), ())), preferred_element_type=jnp.float32)

    count = left[0].shape[0]
    both = one(jnp.concatenate(left, axis=0), right[0])
    return both[:count] + (one(left[0], right[1]) + both[count:])


def fold(tiles):
    count = len(tiles) // 2
    mirrored = [reverse_lanes(tiles[-1 - j], LANES) for j in range(count)]
    return (
        [tiles[j] + mirrored[j] for j in range(count)],
        [tiles[j] - mirrored[j] for j in range(count)],
    )


def reverse_lanes(value, span):
    lane = lax.broadcasted_iota(jnp.int32, value.shape, 1)
    source = lane // span * span + (span - 1) - lane % span
    return jnp.take_along_axis(value, source, axis=1)


def forward_y(
    source, narrow_hbm, full_hbm, out_hbm, rows, narrow, full, out, sem, table_sem, out_sem
):
    points = rows.shape[1]
    half = points // 2
    quarter = half // 2
    fetch = pltpu.make_async_copy(source, rows, sem)
    fetch.start()

    def table_copy(i, from_ref, to_ref):
        at = pl.ds(pl.multiple_of((i % 2) * half, half), half)
        return pltpu.make_async_copy(from_ref.at[at, :], to_ref.at[at, :], table_sem.at[i])

    @pl.loop(0, 2)
    def _(i):
        table_copy(i, narrow_hbm, narrow).start()

    @pl.loop(2, 4)
    def _(i):
        table_copy(i, full_hbm, full).start()

    fetch.wait()
    even, odd = fold([rows[:, pl.ds(j * LANES, LANES)] for j in range(points // LANES)])
    parts = [split(jnp.concatenate(tiles, axis=1)) for tiles in (*fold(even), odd, odd)]
    copies = []
    for i in range(4):
        from_ref, to_ref = (narrow_hbm, narrow) if i < 2 else (full_hbm, full)
        if i % 2 == 0:
            table_copy(i, from_ref, to_ref).wait()
            table_copy(i + 1, from_ref, to_ref).wait()
        high = pl.ds((i % 2) * quarter, quarter)
        low = pl.ds(half + (i % 2) * quarter, quarter)
        at = pl.ds(i * quarter, quarter)
        out[at, :] = product((to_ref[high, :], to_ref[low, :]), parts[i], NT)
        copies.append(pltpu.make_async_copy(out.at[at, :], out_hbm.at[at, :], out_sem.at[i]))
        copies[-1].start()
    for copy in copies:
        copy.wait()


def permute(value, source):
    return jnp.take_along_axis(value, source, axis=1)


def exchange(a, b, keep, source, turn=None):
    moved = jnp.where(keep, b, a)
    moved = pltpu.roll(moved, LANES // 2, 1) if source is None else permute(moved, source)
    if turn is None:
        return jnp.where(keep, a, moved), jnp.where(keep, moved, b)
    kept = permute(jnp.where(keep, a, b), turn)
    return jnp.where(keep, kept, moved), jnp.where(keep, moved, kept)


def swap_groups(v, lane, reverse):
    keep = lane < 2 * GROUP
    t0, t2 = exchange(v[0], v[2], keep, None)
    t1, t3 = exchange(v[1], v[3], keep, None)
    keep = lane // GROUP % 2 == 0
    w = exchange(t0, t1, keep, lane ^ GROUP) + exchange(t2, t3, keep, lane ^ GROUP)
    if reverse:
        w = tuple(permute(x, lane ^ (GROUP - 1)) for x in w)
    return w


def wide(row, width):
    return jnp.concatenate([jnp.broadcast_to(row, (SUB, LANES))] * (width // LANES), axis=1)


def conductances(h):
    zero = jnp.zeros_like(h[0])
    padded = [zero] + h + [zero]
    return [2.0 / (padded[i] + padded[i + 1]) for i in range(len(h) + 1)]


def pivots(own, next1, next2, next3, heights, inverse):
    slab = own.shape[0]
    slabs = 4
    depth = slab * slabs
    width = inverse.shape[1]
    grow = lax.axis_index("growth")
    rank = grow * lax.axis_size("lat") + lax.axis_index("lat")
    for k, ref in enumerate((own, next1, next2, next3)):
        at = pl.ds(pl.multiple_of(lax.rem(grow + k, slabs) * slab, slab), slab)
        heights[at, :] = ref[...]
    row = lax.broadcasted_iota(jnp.int32, (SUB, LANES), 0) + rank * SUB
    column = lax.broadcasted_iota(jnp.int32, (SUB, width), 1)
    ey = jnp.concatenate([eigenvalue(row, width)] * (width // LANES), axis=1)
    total = ey + eigenvalue(column, width)
    h = [heights[z : z + 1, :] for z in range(depth)]
    conduct = conductances(h)
    inv = None
    for z in range(depth):
        pivot = wide(conduct[z] + conduct[z + 1], width) + wide(h[z], width) * total
        if z:
            pivot = pivot - wide(conduct[z] * conduct[z], width) * inv
        inv = 1.0 / pivot
        inverse[pl.ds(z * SUB, SUB), :] = inv


def middle(
    moved, narrow, full, own, next1, next2, next3, out, rows, modal, heights, inverse
):
    slabs = 4
    pivots(own, next1, next2, next3, heights, inverse)
    depth = heights.shape[0]
    slab = depth // slabs
    lat = moved.shape[0] // slabs
    width = rows.shape[1]
    half = width // 2
    quarter = half // 2
    tiles = half // LANES
    lane = lax.broadcasted_iota(jnp.int32, (SUB, LANES), 1)
    chunks = 2
    span = half // chunks
    blocks = [(g, s) for g in range(slabs) for s in range(2)]

    def place(g, s, q):
        return pl.ds((g * slab + s * 4 + q) * SUB, SUB)

    def narrow_part(which):
        return (
            narrow[pl.ds(which * quarter, quarter), :],
            narrow[pl.ds(half + which * quarter, quarter), :],
        )

    def full_part(c):
        at = pl.ds(c * span, span)
        return full[pl.ds(0, half), at], full[pl.ds(half, half), at]

    for c in range(chunks):
        for g, s in blocks:
            lanes = pl.ds(s * LANES, LANES)
            for j in range(c * tiles // chunks, (c + 1) * tiles // chunks):
                first = swap_groups(
                    [moved[g * lat + 4 * j + i, :, lanes] for i in range(4)], lane, False
                )
                second = swap_groups(
                    [moved[g * lat + lat - 1 - 4 * j - i, :, lanes] for i in range(4)],
                    lane,
                    True,
                )
                for q in range(4):
                    at = place(g, s, q)
                    rows[at, pl.ds(j * LANES, LANES)] = first[q] + second[q]
                    rows[at, pl.ds(half + j * LANES, LANES)] = first[q] - second[q]
        data = split(rows[:, pl.ds(half + c * span, span)])
        value = shared(data, full_part(c), NT)
        to = pl.ds(half, half)
        modal[:, to] = value if c == 0 else modal[:, to] + value
    for g, s in blocks:
        for q in range(4):
            at = place(g, s, q)
            even = fold([rows[at, pl.ds(j * LANES, LANES)] for j in range(tiles)])
            for j, tile in enumerate(even[0] + even[1]):
                rows[at, pl.ds(j * LANES, LANES)] = tile
    for which in range(2):
        at = pl.ds(which * quarter, quarter)
        modal[:, at] = shared(split(rows[:, at]), narrow_part(which), NT)

    h = [heights[z : z + 1, :] for z in range(depth)]
    conduct = conductances(h)

    def solve(which):
        lanes = pl.ds(which * half, half)
        partial = None
        for z in range(depth):
            at = pl.ds(z * SUB, SUB)
            value = wide(h[z], half) * modal[at, lanes]
            if z:
                value = value + wide(conduct[z], half) * partial
            partial = value * inverse[at, lanes]
            modal[at, lanes] = partial
        solved = partial
        for z in reversed(range(depth - 1)):
            at = pl.ds(z * SUB, SUB)
            solved = modal[at, lanes] + wide(conduct[z + 1], half) * inverse[at, lanes] * solved
            modal[at, lanes] = solved

    solve(1)
    odd = split(modal[:, pl.ds(half, half)])
    for c in range(chunks):
        rows[:, pl.ds(half + c * span, span)] = shared(odd, full_part(c), NN)
    solve(0)
    for which in range(2):
        at = pl.ds(which * quarter, quarter)
        rows[:, at] = shared(split(modal[:, at]), narrow_part(which), NN)
    for g, s in blocks:
        for q in range(4):
            at = place(g, s, q)
            tile = [rows[at, pl.ds(j * LANES, LANES)] for j in range(tiles)]
            count = tiles // 2
            for j in range(count):
                rows[at, pl.ds(j * LANES, LANES)] = tile[j] + tile[count + j]
                rows[at, pl.ds((tiles - 1 - j) * LANES, LANES)] = reverse_lanes(
                    tile[j] - tile[count + j], LANES
                )
    for c in range(chunks):
        for g, s in blocks:
            lanes = pl.ds(s * LANES, LANES)
            for j in range(c * tiles // chunks, (c + 1) * tiles // chunks):
                first = []
                second = []
                for q in range(4):
                    a = rows[place(g, s, q), pl.ds(j * LANES, LANES)]
                    b = rows[place(g, s, q), pl.ds(half + j * LANES, LANES)]
                    first.append(a + b)
                    second.append(a - b)
                for i, v in enumerate(swap_groups(first, lane, False)):
                    out[g * lat + 4 * j + i, :, lanes] = v
                for i, v in enumerate(swap_groups(second, lane, True)):
                    out[g * lat + lat - 1 - 4 * j - i, :, lanes] = v


def mirror(value):
    count = value.shape[1] // LANES
    return jnp.concatenate(
        [
            reverse_lanes(value[:, (count - 1 - j) * LANES : (count - j) * LANES], LANES)
            for j in range(count)
        ],
        axis=1,
    )


def inverse_y(planes, narrow, full, out, result, sem):
    points = planes.shape[0]
    half = points // 2
    quarter = half // 2
    copies = []

    def send(start):
        at = pl.ds(start, quarter)
        copies.append(
            pltpu.make_async_copy(result.at[:, at], out.at[:, at], sem.at[len(copies)])
        )
        copies[-1].start()

    sums, differences = (
        shared(
            split(planes[pl.ds(which * quarter, quarter), :].T),
            (
                narrow[pl.ds(which * quarter, quarter), :],
                narrow[pl.ds(half + which * quarter, quarter), :],
            ),
            NN,
        )
        for which in range(2)
    )
    data = split(planes[pl.ds(half, half), :].T)
    for c in range(2):
        at = pl.ds(c * quarter, quarter)
        odd = shared(data, (full[pl.ds(0, half), at], full[pl.ds(half, half), at]), NN)
        even = sums + differences if c == 0 else mirror(sums - differences)
        result[:, at] = even + odd
        send(c * quarter)
        other = points - (c + 1) * quarter
        result[:, pl.ds(other, quarter)] = mirror(even - odd)
        send(other)
    for copy in copies:
        copy.wait()


VMEM = pl.BlockSpec(memory_space=pltpu.VMEM)
HBM = pl.BlockSpec(memory_space=pltpu.HBM)


def shape(*dims, dtype=jnp.float32):
    return jax.ShapeDtypeStruct(dims, dtype)


FULL = 67043328


def limit(size):
    return pltpu.CompilerParams(vmem_limit_bytes=size)


def solution(mesh):
    slabs = mesh.shape["growth"]
    lat = mesh.shape["lat"]

    def per_device(source, spacing):
        slab, xlocal, width = source.shape
        devices = slabs * lat
        flat = slab * xlocal
        half = width // 2
        depth = slab * slabs
        narrow, full = (jnp.asarray(a) for a in tables(width))
        own = jnp.broadcast_to(spacing[:, None], (slab, LANES))
        others = [
            lax.ppermute(own, "growth", [((j + k) % slabs, j) for j in range(slabs)])
            for k in range(1, slabs)
        ]
        planes = pl.pallas_call(
            forward_y,
            out_shape=shape(width, flat),
            in_specs=[HBM, HBM, HBM],
            out_specs=HBM,
            scratch_shapes=[
                pltpu.VMEM((flat, width), jnp.float32),
                pltpu.VMEM((width, half // 2), jnp.bfloat16),
                pltpu.VMEM((width, half), jnp.bfloat16),
                pltpu.VMEM((width, flat), jnp.float32),
                pltpu.SemaphoreType.DMA,
                pltpu.SemaphoreType.DMA((4,)),
                pltpu.SemaphoreType.DMA((4,)),
            ],
            compiler_params=limit(FULL),
            name="forward_y",
        )(source.reshape(flat, width), narrow, full)
        moved = lax.all_to_all(planes.reshape(devices, SUB, flat), ALL, 0, 0, tiled=True)
        spatial = pl.pallas_call(
            middle,
            out_shape=shape(devices, SUB, flat),
            in_specs=[VMEM] * 7,
            out_specs=VMEM,
            scratch_shapes=[
                pltpu.VMEM((depth * SUB, width), jnp.float32),
                pltpu.VMEM((depth * SUB, width), jnp.float32),
                pltpu.VMEM((depth, LANES), jnp.float32),
                pltpu.VMEM((depth * SUB, width), jnp.float32),
            ],
            compiler_params=limit(24 << 20),
            name="middle",
        )(moved, narrow, full, own, *others)
        returned = lax.all_to_all(spatial, ALL, 0, 0, tiled=True)
        result = pl.pallas_call(
            inverse_y,
            out_shape=shape(flat, width),
            in_specs=[VMEM] * 3,
            out_specs=HBM,
            scratch_shapes=[
                pltpu.VMEM((flat, width), jnp.float32),
                pltpu.SemaphoreType.DMA((4,)),
            ],
            compiler_params=limit(24 << 20),
            name="inverse_y",
        )(returned.reshape(width, flat), narrow, full)
        return result.reshape(slab, xlocal, width)

    return jax.shard_map(
        per_device,
        mesh=mesh,
        in_specs=(P("growth", "lat", None), P("growth")),
        out_specs=P("growth", "lat", None),
        check_vma=False,
    )
```

```python
import math

import jax
import jax.numpy as jnp
import numpy as np
from jax import lax
from jax.experimental import pallas as pl
from jax.experimental.pallas import tpu as pltpu
from jax.sharding import PartitionSpec as P

ALL = ("growth", "lat")
LANES = 128
SUB = 8
GROUP = 32
NT = ((1,), (1,))
NN = ((1,), (0,))


def mode_order(points):
    return np.concatenate(
        [np.arange(0, points, 4), np.arange(2, points, 4), np.arange(1, points, 2)]
    )


def part_table(points, modes, columns):
    k = modes[:, None].astype(np.int64)
    j = np.arange(columns, dtype=np.int64)[None, :]
    angle = ((2 * j + 1) * k % (4 * points)).astype(np.float64) * (math.pi / (2.0 * points))
    scale = np.where(k == 0, math.sqrt(1.0 / points), math.sqrt(2.0 / points))
    table = (scale * np.cos(angle)).astype(np.float32)
    high = table.astype(jnp.bfloat16)
    low = (table - high.astype(np.float32)).astype(jnp.bfloat16)
    return np.concatenate([high, low], axis=0)


def tables(points):
    modes = mode_order(points)
    half = points // 2
    return part_table(points, modes[:half], half // 2), part_table(points, modes[half:], half)


def quarter_sine(angle):
    square = angle * angle
    value = 1.0 - square * (1.0 / 156.0)
    for divisor in (110.0, 72.0, 42.0, 20.0, 6.0):
        value = 1.0 - square * value * (1.0 / divisor)
    return angle * value


def eigenvalue(slot, points):
    half = points // 2
    quarter = points // 4
    even = jnp.where(slot < quarter, 4 * slot, 4 * (slot - quarter) + 2)
    mode = jnp.where(slot < half, even, 2 * (slot - half) + 1)
    sine = quarter_sine(mode.astype(jnp.float32) * (math.pi / (2.0 * points)))
    return 4.0 * sine * sine


def split(value):
    high = value.astype(jnp.bfloat16)
    low = (value - high.astype(jnp.float32)).astype(jnp.bfloat16)
    return high, low


def product(left, right, dims):
    def one(a, b):
        return lax.dot_general(a, b, (dims, ((), ())), preferred_element_type=jnp.float32)

    return one(left[0], right[0]) + (one(left[0], right[1]) + one(left[1], right[0]))


def shared(left, right, dims):
    def one(a, b):
        return lax.dot_general(a, b, (dims, ((), ())), preferred_element_type=jnp.float32)

    count = left[0].shape[0]
    both = one(jnp.concatenate(left, axis=0), right[0])
    return both[:count] + (one(left[0], right[1]) + both[count:])


def fold(tiles):
    count = len(tiles) // 2
    mirrored = [reverse_lanes(tiles[-1 - j], LANES) for j in range(count)]
    return (
        [tiles[j] + mirrored[j] for j in range(count)],
        [tiles[j] - mirrored[j] for j in range(count)],
    )


def reverse_lanes(value, span):
    lane = lax.broadcasted_iota(jnp.int32, value.shape, 1)
    source = lane // span * span + (span - 1) - lane % span
    return jnp.take_along_axis(value, source, axis=1)


def turned_cells(slab):
    own = lax.rem(lax.axis_index("lat"), 4)
    cells = [4 * (p // 4) + lax.rem(p % 4 + 4 - own, 4) for p in range(slab)]
    return [pl.multiple_of(cell * GROUP, GROUP) for cell in cells]


def forward_y(
    source, narrow_hbm, full_hbm, out_hbm, rows, narrow, full, out, sem, table_sem, out_sem
):
    points = rows.shape[1]
    half = points // 2
    quarter = half // 2
    fetch = pltpu.make_async_copy(source, rows, sem)
    fetch.start()

    def table_copy(i, from_ref, to_ref):
        at = pl.ds(pl.multiple_of((i % 2) * half, half), half)
        return pltpu.make_async_copy(from_ref.at[at, :], to_ref.at[at, :], table_sem.at[i])

    @pl.loop(0, 2)
    def _(i):
        table_copy(i, narrow_hbm, narrow).start()

    @pl.loop(2, 4)
    def _(i):
        table_copy(i, full_hbm, full).start()

    fetch.wait()
    starts = turned_cells(rows.shape[0] // GROUP)

    def column(j):
        lanes = pl.ds(j * LANES, LANES)
        return jnp.concatenate([rows[pl.ds(at, GROUP), lanes] for at in starts], axis=0)

    even, odd = fold([column(j) for j in range(points // LANES)])
    parts = [split(jnp.concatenate(tiles, axis=1)) for tiles in (*fold(even), odd, odd)]
    copies = []
    for i in range(4):
        from_ref, to_ref = (narrow_hbm, narrow) if i < 2 else (full_hbm, full)
        if i % 2 == 0:
            table_copy(i, from_ref, to_ref).wait()
            table_copy(i + 1, from_ref, to_ref).wait()
        high = pl.ds((i % 2) * quarter, quarter)
        low = pl.ds(half + (i % 2) * quarter, quarter)
        at = pl.ds(i * quarter, quarter)
        out[at, :] = product((to_ref[high, :], to_ref[low, :]), parts[i], NT)
        copies.append(pltpu.make_async_copy(out.at[at, :], out_hbm.at[at, :], out_sem.at[i]))
        copies[-1].start()
    for copy in copies:
        copy.wait()


def pick(tiles, lane):
    group = lane // GROUP
    upper = jnp.where(group == 2, tiles[2], tiles[3])
    return jnp.where(group < 2, jnp.where(group == 0, tiles[0], tiles[1]), upper)


def turn(value, count):
    return pltpu.roll(value, GROUP * (count % 4), 1) if count % 4 else value


def collect(v, lane, reverse):
    if not reverse:
        return [turn(pick([v[(p - q) % 4] for p in range(4)], lane), -q) for q in range(4)]
    picked = [pick([v[(q + 3 - p) % 4] for p in range(4)], lane) for q in range(4)]
    return [turn(reverse_lanes(tile, LANES), q) for q, tile in enumerate(picked)]


def spread(w, lane, reverse):
    if not reverse:
        turned = [turn(tile, q) for q, tile in enumerate(w)]
        return [pick([turned[(p - i) % 4] for p in range(4)], lane) for i in range(4)]
    turned = [reverse_lanes(turn(tile, -q), LANES) for q, tile in enumerate(w)]
    return [pick([turned[(i + p + 1) % 4] for p in range(4)], lane) for i in range(4)]


def wide(row, width):
    return jnp.concatenate([jnp.broadcast_to(row, (SUB, LANES))] * (width // LANES), axis=1)


def conductances(h):
    zero = jnp.zeros_like(h[0])
    padded = [zero] + h + [zero]
    return [2.0 / (padded[i] + padded[i + 1]) for i in range(len(h) + 1)]


def pivots(own, next1, next2, next3, heights, inverse):
    slab = own.shape[0]
    slabs = 4
    depth = slab * slabs
    width = inverse.shape[1]
    grow = lax.axis_index("growth")
    rank = grow * lax.axis_size("lat") + lax.axis_index("lat")
    for k, ref in enumerate((own, next1, next2, next3)):
        at = pl.ds(pl.multiple_of(lax.rem(grow + k, slabs) * slab, slab), slab)
        heights[at, :] = ref[...]
    row = lax.broadcasted_iota(jnp.int32, (SUB, LANES), 0) + rank * SUB
    column = lax.broadcasted_iota(jnp.int32, (SUB, width), 1)
    ey = jnp.concatenate([eigenvalue(row, width)] * (width // LANES), axis=1)
    total = ey + eigenvalue(column, width)
    h = [heights[z : z + 1, :] for z in range(depth)]
    conduct = conductances(h)
    inv = None
    for z in range(depth):
        pivot = wide(conduct[z] + conduct[z + 1], width) + wide(h[z], width) * total
        if z:
            pivot = pivot - wide(conduct[z] * conduct[z], width) * inv
        inv = 1.0 / pivot
        inverse[pl.ds(z * SUB, SUB), :] = inv


def middle(
    moved, narrow, full, own, next1, next2, next3, out, rows, modal, heights, inverse
):
    slabs = 4
    pivots(own, next1, next2, next3, heights, inverse)
    depth = heights.shape[0]
    slab = depth // slabs
    lat = moved.shape[0] // slabs
    width = rows.shape[1]
    half = width // 2
    quarter = half // 2
    tiles = half // LANES
    lane = lax.broadcasted_iota(jnp.int32, (SUB, LANES), 1)
    chunks = 2
    span = half // chunks
    blocks = [(g, s) for g in range(slabs) for s in range(2)]

    def place(g, s, q):
        return pl.ds((g * slab + s * 4 + q) * SUB, SUB)

    def narrow_part(which):
        return (
            narrow[pl.ds(which * quarter, quarter), :],
            narrow[pl.ds(half + which * quarter, quarter), :],
        )

    def full_part(c):
        at = pl.ds(c * span, span)
        return full[pl.ds(0, half), at], full[pl.ds(half, half), at]

    for c in range(chunks):
        for g, s in blocks:
            lanes = pl.ds(s * LANES, LANES)
            for j in range(c * tiles // chunks, (c + 1) * tiles // chunks):
                first = collect(
                    [moved[g * lat + 4 * j + i, :, lanes] for i in range(4)], lane, False
                )
                second = collect(
                    [moved[g * lat + lat - 1 - 4 * j - i, :, lanes] for i in range(4)],
                    lane,
                    True,
                )
                for q in range(4):
                    at = place(g, s, q)
                    rows[at, pl.ds(j * LANES, LANES)] = first[q] + second[q]
                    rows[at, pl.ds(half + j * LANES, LANES)] = first[q] - second[q]
        data = split(rows[:, pl.ds(half + c * span, span)])
        value = shared(data, full_part(c), NT)
        to = pl.ds(half, half)
        modal[:, to] = value if c == 0 else modal[:, to] + value
    for g, s in blocks:
        for q in range(4):
            at = place(g, s, q)
            even = fold([rows[at, pl.ds(j * LANES, LANES)] for j in range(tiles)])
            for j, tile in enumerate(even[0] + even[1]):
                rows[at, pl.ds(j * LANES, LANES)] = tile
    for which in range(2):
        at = pl.ds(which * quarter, quarter)
        modal[:, at] = shared(split(rows[:, at]), narrow_part(which), NT)

    h = [heights[z : z + 1, :] for z in range(depth)]
    conduct = conductances(h)

    def solve(which):
        lanes = pl.ds(which * half, half)
        partial = None
        for z in range(depth):
            at = pl.ds(z * SUB, SUB)
            value = wide(h[z], half) * modal[at, lanes]
            if z:
                value = value + wide(conduct[z], half) * partial
            partial = value * inverse[at, lanes]
            modal[at, lanes] = partial
        solved = partial
        for z in reversed(range(depth - 1)):
            at = pl.ds(z * SUB, SUB)
            solved = modal[at, lanes] + wide(conduct[z + 1], half) * inverse[at, lanes] * solved
            modal[at, lanes] = solved

    solve(1)
    odd = split(modal[:, pl.ds(half, half)])
    for c in range(chunks):
        rows[:, pl.ds(half + c * span, span)] = shared(odd, full_part(c), NN)
    solve(0)
    for which in range(2):
        at = pl.ds(which * quarter, quarter)
        rows[:, at] = shared(split(modal[:, at]), narrow_part(which), NN)
    for g, s in blocks:
        for q in range(4):
            at = place(g, s, q)
            tile = [rows[at, pl.ds(j * LANES, LANES)] for j in range(tiles)]
            count = tiles // 2
            for j in range(count):
                rows[at, pl.ds(j * LANES, LANES)] = tile[j] + tile[count + j]
                rows[at, pl.ds((tiles - 1 - j) * LANES, LANES)] = reverse_lanes(
                    tile[j] - tile[count + j], LANES
                )
    for c in range(chunks):
        for g, s in blocks:
            lanes = pl.ds(s * LANES, LANES)
            for j in range(c * tiles // chunks, (c + 1) * tiles // chunks):
                first = []
                second = []
                for q in range(4):
                    a = rows[place(g, s, q), pl.ds(j * LANES, LANES)]
                    b = rows[place(g, s, q), pl.ds(half + j * LANES, LANES)]
                    first.append(a + b)
                    second.append(a - b)
                for i, v in enumerate(spread(first, lane, False)):
                    out[g * lat + 4 * j + i, :, lanes] = v
                for i, v in enumerate(spread(second, lane, True)):
                    out[g * lat + lat - 1 - 4 * j - i, :, lanes] = v


def mirror(value):
    count = value.shape[1] // LANES
    return jnp.concatenate(
        [
            reverse_lanes(value[:, (count - 1 - j) * LANES : (count - j) * LANES], LANES)
            for j in range(count)
        ],
        axis=1,
    )


def inverse_y(planes, narrow, full, out, result, sem):
    points = planes.shape[0]
    half = points // 2
    quarter = half // 2
    copies = []

    starts = turned_cells(result.shape[0] // GROUP)

    def send(start, value):
        at = pl.ds(start, quarter)
        for p, row in enumerate(starts):
            result[pl.ds(row, GROUP), at] = value[p * GROUP : (p + 1) * GROUP, :]
        copies.append(
            pltpu.make_async_copy(result.at[:, at], out.at[:, at], sem.at[len(copies)])
        )
        copies[-1].start()

    sums, differences = (
        shared(
            split(planes[pl.ds(which * quarter, quarter), :].T),
            (
                narrow[pl.ds(which * quarter, quarter), :],
                narrow[pl.ds(half + which * quarter, quarter), :],
            ),
            NN,
        )
        for which in range(2)
    )
    data = split(planes[pl.ds(half, half), :].T)
    for c in range(2):
        at = pl.ds(c * quarter, quarter)
        odd = shared(data, (full[pl.ds(0, half), at], full[pl.ds(half, half), at]), NN)
        even = sums + differences if c == 0 else mirror(sums - differences)
        send(c * quarter, even + odd)
        send(points - (c + 1) * quarter, mirror(even - odd))
    for copy in copies:
        copy.wait()


VMEM = pl.BlockSpec(memory_space=pltpu.VMEM)
HBM = pl.BlockSpec(memory_space=pltpu.HBM)


def shape(*dims, dtype=jnp.float32):
    return jax.ShapeDtypeStruct(dims, dtype)


FULL = 67043328


def limit(size):
    return pltpu.CompilerParams(vmem_limit_bytes=size)


def solution(mesh):
    slabs = mesh.shape["growth"]
    lat = mesh.shape["lat"]

    def per_device(source, spacing):
        slab, xlocal, width = source.shape
        devices = slabs * lat
        flat = slab * xlocal
        half = width // 2
        depth = slab * slabs
        narrow, full = (jnp.asarray(a) for a in tables(width))
        own = jnp.broadcast_to(spacing[:, None], (slab, LANES))
        others = [
            lax.ppermute(own, "growth", [((j + k) % slabs, j) for j in range(slabs)])
            for k in range(1, slabs)
        ]
        planes = pl.pallas_call(
            forward_y,
            out_shape=shape(width, flat),
            in_specs=[HBM, HBM, HBM],
            out_specs=HBM,
            scratch_shapes=[
                pltpu.VMEM((flat, width), jnp.float32),
                pltpu.VMEM((width, half // 2), jnp.bfloat16),
                pltpu.VMEM((width, half), jnp.bfloat16),
                pltpu.VMEM((width, flat), jnp.float32),
                pltpu.SemaphoreType.DMA,
                pltpu.SemaphoreType.DMA((4,)),
                pltpu.SemaphoreType.DMA((4,)),
            ],
            compiler_params=limit(FULL),
            name="forward_y",
        )(source.reshape(flat, width), narrow, full)
        moved = lax.all_to_all(planes.reshape(devices, SUB, flat), ALL, 0, 0, tiled=True)
        spatial = pl.pallas_call(
            middle,
            out_shape=shape(devices, SUB, flat),
            in_specs=[VMEM] * 7,
            out_specs=VMEM,
            scratch_shapes=[
                pltpu.VMEM((depth * SUB, width), jnp.float32),
                pltpu.VMEM((depth * SUB, width), jnp.float32),
                pltpu.VMEM((depth, LANES), jnp.float32),
                pltpu.VMEM((depth * SUB, width), jnp.float32),
            ],
            compiler_params=limit(24 << 20),
            name="middle",
        )(moved, narrow, full, own, *others)
        returned = lax.all_to_all(spatial, ALL, 0, 0, tiled=True)
        result = pl.pallas_call(
            inverse_y,
            out_shape=shape(flat, width),
            in_specs=[VMEM] * 3,
            out_specs=HBM,
            scratch_shapes=[
                pltpu.VMEM((flat, width), jnp.float32),
                pltpu.SemaphoreType.DMA((4,)),
            ],
            compiler_params=limit(24 << 20),
            name="inverse_y",
        )(returned.reshape(width, flat), narrow, full)
        return result.reshape(slab, xlocal, width)

    return jax.shard_map(
        per_device,
        mesh=mesh,
        in_specs=(P("growth", "lat", None), P("growth")),
        out_specs=P("growth", "lat", None),
        check_vma=False,
    )
```
